32 devices in a mesh: pole: 4 (over y, x), blk: 8 (over z, core).
Axes of the slice: x: 2, y: 2, z: 4, core: 2. Of those that a mesh axis runs over, the one named last changes fastest.
Arguments:
- inverse_blocks: bfloat16 [8, 8192, 256], P('pole', 'blk'), may hold values from -6 to 6
- panel_blocks: bfloat16 [8, 1024, 1024], P('pole', 'blk'), may hold values from -0.125 to 0.125
- ancestor_mask: int32 [8, 4], P('blk'), may hold values 0 or 1
- diag_inverse: float32 [8, 512, 256], P('pole', 'blk'), may hold values from -6 to 6
- pole_weights: float32 [8, 2], replicated, may hold values from -6 to 6
- pole_order: int32 [8], replicated, may hold values from 0 to 7, each once
Outputs:
- density_columns: float32 [1024, 512], P('blk', 'pole')
- density_diag: float32 [512, 128], P('blk', 'pole')
The draws below stay inside these ranges and needn't reach their ends.
Inputs may be any that keep to these rules, and one draw needn't show every extreme that they name: `pole_order`: each data position names a different pole number.
All inputs are finite; a program needn't handle non-finite values. No bound on the sum of `ancestor_mask` on one device may be relied on, other than what follows from the above.
Results may differ from the reference program's by a relative error of at most 0.0003.
Values may be sent and summed in bfloat16 or wider, within the bound.
A program may use at most 128 MiB of HBM per device.

```python
import jax
import jax.numpy as jnp
from jax import lax

W = 128
S = 4
PC = 8
POLES = 8
NA = 8
PR = 1
N_BLK = 8


def plant(values, key, low, high):
    shape = values.shape
    index_at = [jax.random.randint(jax.random.fold_in(key, axis), (), 0, shape[axis]) for axis in range(len(shape))]
    values = values.at[tuple(index_at)].set(low)
    longest = shape.index(max(shape))
    index_at[longest] = (index_at[longest] + 1) % shape[longest]
    return values.at[tuple(index_at)].set(high)


def level_of(stream_key, dims, pieces, low, largest):
    def one(axis_at, blocks):
        draws = jax.random.uniform(jax.random.fold_in(jax.random.fold_in(stream_key, 6), axis_at), (blocks,), jnp.float32, low / len(pieces), largest / len(pieces))
        return jnp.repeat(jnp.exp(draws), dims[axis_at] // blocks).reshape((-1,) + (1,) * (len(dims) - axis_at - 1))

    loudness = one(*pieces[0])
    for cut in pieces[1:]:
        loudness = loudness * one(*cut)
    return loudness


def bell_draw(stream_key, shape, width, reach, pieces=(), kind=jnp.bfloat16):
    level = level_of(stream_key, shape, pieces, -0.22, 0.18) if pieces else 1.0
    values = jax.random.normal(stream_key, shape, jnp.float32) * width * level
    return jnp.minimum(jnp.maximum(values, -reach), reach).astype(kind)


def setup_inputs(seed: int = 0) -> dict:
    keys = jax.random.split(jax.random.key(seed), 7)
    inverse_blocks = bell_draw(keys[0], (POLES, N_BLK * PC * W, PR * 2 * W), 1.0, 6.0, ((0, 4), (1, 8)))
    panel_blocks = bell_draw(keys[1], (POLES, NA * W, 2 * S * W), (2 * W * NA) ** -0.5, 0.125, ((0, 4), (1, 8)))
    ancestor_mask = plant((jax.random.randint(keys[2], (NA, S), 0, 4) < 3).astype(jnp.int32), jax.random.fold_in(keys[2], 1), 0, 1)
    diag_inverse = bell_draw(keys[3], (POLES, S * W, 2 * W), 1.0, 6.0, ((0, 4), (1, 8)), jnp.float32)
    pole_weights = bell_draw(keys[4], (POLES, 2), 1.0, 6.0, (), jnp.float32)
    pole_order = jax.random.permutation(keys[5], POLES).astype(jnp.int32)
    return dict(inverse_blocks=inverse_blocks, panel_blocks=panel_blocks, ancestor_mask=ancestor_mask, diag_inverse=diag_inverse, pole_weights=pole_weights, pole_order=pole_order)


def trace_parts(left_real, left_imag, right_real, right_imag):
    form = "iukx,iuky->kxy"
    high = lax.Precision.HIGHEST
    real_part = jnp.einsum(form, left_real, right_real, precision=high) - jnp.einsum(form, left_imag, right_imag, precision=high)
    imag_part = jnp.einsum(form, left_real, right_imag, precision=high) + jnp.einsum(form, left_imag, right_real, precision=high)
    return real_part, imag_part


def reference(inverse_blocks, panel_blocks, ancestor_mask, diag_inverse, pole_weights, pole_order):
    span = S * W
    mask_bf = ancestor_mask.astype(jnp.bfloat16)[:, None, None, :, None]
    mask_f = ancestor_mask.astype(jnp.float32)
    density_sum = jnp.zeros((NA, W, S, W), jnp.float32)
    diag_sum = jnp.zeros((S, W, W), jnp.float32)
    for position in range(POLES):
        pole_id = pole_order[position]
        weight_real = pole_weights[pole_id, 0]
        weight_imag = pole_weights[pole_id, 1]
        masked = (panel_blocks[position].reshape(NA, W, 2, S, W) * mask_bf).reshape(NA, W, 2 * span)
        blocks = masked.reshape(PR, PC, W, 2 * span)
        lower_rows = jnp.concatenate([-blocks[..., span:], blocks[..., :span]], axis=-1)
        real_form = jnp.concatenate([blocks, lower_rows], axis=2)
        inverse_mat = inverse_blocks[position].reshape(PR, PC, PC * W, PR, 2 * W)
        selected = -jnp.einsum("rbmas,absn->rmn", inverse_mat.astype(jnp.float32), real_form.astype(jnp.float32))
        selected = selected.reshape(NA, W, 2, S, W)
        sel_real = selected[:, :, 0]
        sel_imag = selected[:, :, 1]
        density_sum = density_sum + weight_real * sel_real - weight_imag * sel_imag
        panel_f = masked.astype(jnp.float32).reshape(NA, W, 2, S, W)
        term_real, term_imag = trace_parts(panel_f[:, :, 0], panel_f[:, :, 1], sel_real, sel_imag)
        diag_blocks = diag_inverse[position].reshape(S, W, 2 * W)
        diag_sum = diag_sum + weight_real * (diag_blocks[..., :W] - term_real) - weight_imag * (diag_blocks[..., W:] - term_imag)
    density_sum = density_sum * mask_f[:, None, :, None]
    return density_sum.reshape(NA * W, span), diag_sum.reshape(span, W)
```

```python
import functools

import jax
import jax.numpy as jnp
from jax import lax
from jax.experimental import pallas as pl
from jax.experimental.pallas import tpu as pltpu
from jax.sharding import PartitionSpec as P

PC = 8
CHIPS = PC // 2
MESH = pl.DeviceIdType.MESH
F32 = jnp.float32
BF16 = jnp.bfloat16


def from_behind(array, axis, by):
    size = lax.axis_size(axis)
    return lax.ppermute(array, axis, [(i, (i + by) % size) for i in range(size)])


def dot00(left, right):
    return lax.dot_general(left, right, (((0,), (0,)), ((), ())), preferred_element_type=F32)


def kernel(cfg, *refs):
    n, rg, local, width, sn = cfg
    span = sn * width
    cw = span // n
    piece = span // (PC * rg)
    refs = list(refs)
    weight_ref, order_ref, mask_ref, inv_ref, own_ref = refs[:5]
    refs = refs[5:]
    col_ref = refs.pop(0) if rg > 1 else None
    diag_ref, dens_ref, dout_ref = refs[:3]
    (lall, gram, wfull, wrecv, wacc, wpole, wsum, wz, tbuf, trecv, tacc, tz, tsum, tpole,
     ss_z, ss_p, rs_z, rs_p, ss_wp, rs_wp, ss_wq, rs_wq, ss_wz, rs_wz,
     ss_tp, rs_tp, ss_tz, rs_tz, ss_tq, rs_tq) = refs[3:]

    me = lax.axis_index("blk")
    q = lax.axis_index("pole")
    rank = lax.rem(me, PC)
    first = me - rank
    z = rank // 2
    core = lax.rem(rank, 2)
    other = 1 - core

    def device(chip, which, pole):
        return {"pole": pole, "blk": first + 2 * chip + which}

    partner = device(z, other, q)

    def remote(src, dst, send, recv, where):
        return pltpu.make_async_remote_copy(
            src_ref=src, dst_ref=dst, send_sem=send, recv_sem=recv,
            device_id=where, device_id_type=MESH)

    peers = [partner]
    peers += [device(lax.rem(z + o, CHIPS), core, q) for o in range(1, CHIPS)]
    peers += [device(z, core, lax.rem(q + o, n)) for o in range(1, n)]
    barrier = pltpu.get_barrier_semaphore()
    for peer in peers:
        pl.semaphore_signal(barrier, inc=1, device_id=peer, device_id_type=MESH)
    pl.semaphore_wait(barrier, len(peers))

    def slot(p, chip, which):
        return lall.at[p, pl.ds(pl.multiple_of((2 * chip + which) * width, width), width)]

    def to_chip(src, p, chip, sgn, h):
        return remote(src, slot(p, chip, core), ss_z.at[(1 - sgn) // 2, h, p], rs_z.at[chip, p],
                      device(z + sgn, core, q))

    def to_partner(src, p, chip):
        return remote(src, slot(p, chip, core), ss_p.at[chip, p], rs_p.at[chip, p], partner)

    def inside(chip):
        return jnp.logical_and(chip >= 0, chip < CHIPS)

    for p in range(local):
        for sgn in (1, -1):
            @pl.when(inside(z + sgn))
            def _():
                to_chip(own_ref.at[p], p, z, sgn, 0).start()
    for p in range(local):
        to_partner(own_ref.at[p], p, z).start()

    poles = [order_ref[q * local + p] for p in range(local)]
    w_re = [weight_ref[poles[p], 0] for p in range(local)]
    w_im = [weight_ref[poles[p], 1] for p in range(local)]

    def column(p, a):
        return own_ref.at[p] if rg == 1 else col_ref.at[p, a]

    def part_copy(t):
        return remote(wfull.at[t, :, other], wrecv.at[t], ss_wp.at[t], rs_wp.at[t], partner)

    order = [lax.rem(q + o, n) for o in list(range(1, n)) + [0]]
    for t in order:
        total = None
        for p in range(local):
            product = None
            for a in range(rg):
                block = column(p, a)
                re = block[:, pl.ds(pl.multiple_of(t * cw, 128), cw)]
                im = block[:, pl.ds(pl.multiple_of(span + t * cw, 128), cw)]
                real_form = jnp.concatenate(
                    [jnp.concatenate([re, im], axis=1), jnp.concatenate([-im, re], axis=1)], axis=0)
                term = jnp.dot(inv_ref[p, :, 2 * width * a:2 * width * (a + 1)], real_form,
                               preferred_element_type=F32)
                product = term if product is None else product + term
            term = w_im[p] * product[:, cw:] - w_re[p] * product[:, :cw]
            total = term if total is None else total + term
        wfull[t] = total.reshape(CHIPS, 2, width, cw)
        part_copy(t).start()

    for p in range(local):
        lall[p, pl.ds(pl.multiple_of(rank * width, width), width)] = own_ref[p]

    def hop(h):
        for p in range(local):
            for sgn in (1, -1):
                chip = z - sgn * h

                @pl.when(inside(chip))
                def _():
                    here = slot(p, chip, core)
                    remote(here, here, ss_p.at[chip, p], rs_z.at[chip, p], partner).wait_recv()
                    if h < CHIPS - 1:
                        @pl.when(inside(z + sgn))
                        def _():
                            to_chip(here, p, chip, sgn, h).start()
                    to_partner(here, p, chip).start()

    def accumulate(chip, fresh):
        rows = pl.ds(pl.multiple_of(chip * 2 * width, 2 * width), 2 * width)
        for p in range(local):
            theirs = slot(p, chip, other)
            remote(theirs, theirs, ss_p.at[chip, p], rs_p.at[chip, p], partner).wait_recv()
            for a in range(rg):
                at = slice(2 * width * a, 2 * width * (a + 1))
                term = dot00(inv_ref[p, rows, at], lall[p, rows, :])
                gram[p, at, :] = term if fresh else gram[p, at, :] + term

    def gather(h):
        for sgn in (1, -1):
            chip = z - sgn * h

            @pl.when(inside(chip))
            def _():
                accumulate(chip, False)

    def pole_copy(o):
        to = lax.rem(q + o, n)
        return remote(wacc.at[to], wpole.at[o - 1], ss_wq.at[o - 1], rs_wq.at[o - 1], device(z, core, to))

    def line_copy(src, dst, send, recv, o):
        to = lax.rem(z + o, CHIPS)
        return remote(src.at[to], dst.at[o - 1], send.at[o - 1], recv.at[o - 1], device(to, core, q))

    hop(1)
    for o in list(range(1, n)) + [0]:
        t = lax.rem(q + o, n)
        part_copy(t).wait_recv()
        wacc[t] = wfull[t, :, core] + wrecv[t]
        if o:
            pole_copy(o).start()
    accumulate(z, True)
    gather(1)
    hop(2)
    for o in range(1, n):
        pole_copy(o).wait_recv()
    wsum[...] = wacc[q] + functools.reduce(lambda x, y: x + y, [wpole[o] for o in range(n - 1)])
    for o in range(1, CHIPS):
        line_copy(wsum, wz, ss_wz, rs_wz, o).start()
    gather(2)
    hop(3)
    gather(3)

    per_width = width // piece
    traces = [None] * sn
    for p in range(local):
        for a in range(rg):
            base = 2 * width * a
            upper = gram[p, base:base + width, :]
            lower = gram[p, base + width:base + 2 * width, :]
            m_re = upper[:, :span] - lower[:, span:]
            m_im = lower[:, :span] + upper[:, span:]
            n_re = w_re[p] * m_re - w_im[p] * m_im
            n_im = w_re[p] * m_im + w_im[p] * m_re
            both = jnp.concatenate([n_re, -n_im], axis=0)
            high = both.astype(BF16)
            low = (both - high.astype(F32)).astype(BF16)
            block = column(p, a)
            for k in range(sn):
                at = slice(k * width, (k + 1) * width)
                right = jnp.concatenate([block[:, at], block[:, span + k * width:span + (k + 1) * width]], axis=0)
                term = dot00(high[:, at], right) + dot00(low[:, at], right)
                traces[k] = term if traces[k] is None else traces[k] + term
    for g in range(PC * rg):
        k, off = g // per_width, g % per_width * piece
        tbuf[g % PC // 2, g % 2, g // PC] = traces[k][off:off + piece]
    trace_copy = remote(tbuf.at[:, other], trecv, ss_tp.at[0], rs_tp.at[0], partner)
    trace_copy.start()

    for o in range(1, CHIPS):
        line_copy(wsum, wz, ss_wz, rs_wz, o).wait_recv()
    rows = wsum[z] + functools.reduce(lambda x, y: x + y, [wz[o] for o in range(CHIPS - 1)])
    for j in range(cw // width):
        at = slice(j * width, (j + 1) * width)
        dens_ref[:, at] = rows[:, at] * mask_ref[0, q * (cw // width) + j].astype(F32)

    trace_copy.wait_recv()
    tacc[...] = tbuf[:, core] + trecv[...]
    for o in range(1, CHIPS):
        line_copy(tacc, tz, ss_tz, rs_tz, o).start()
    for o in range(1, CHIPS):
        line_copy(tacc, tz, ss_tz, rs_tz, o).wait_recv()
    summed = tacc[z] + functools.reduce(lambda x, y: x + y, [tz[o] for o in range(CHIPS - 1)])
    if rg > 1:
        dout_ref[...] = summed.reshape(rg * piece, width)
    else:
        summed = summed.reshape(piece, width)
        for p in range(local):
            summed = summed + w_re[p] * diag_ref[p, :, :width] - w_im[p] * diag_ref[p, :, width:]
        tsum[...] = summed

        def last_copy(o):
            return remote(tsum, tpole.at[o - 1], ss_tq.at[o - 1], rs_tq.at[o - 1],
                          device(z, core, lax.rem(q + o, n)))

        for o in range(1, n):
            last_copy(o).start()
        for o in range(1, n):
            last_copy(o).wait_recv()
        summed = summed + functools.reduce(lambda x, y: x + y, [tpole[o] for o in range(n - 1)])
        narrow = width // n
        result = jnp.zeros((piece, narrow), F32)
        for t in range(n):
            result = jnp.where(q == t, summed[:, t * narrow:(t + 1) * narrow], result)
        dout_ref[...] = result
        for o in range(1, n):
            last_copy(o).wait_send()

    for p in range(local):
        to_partner(own_ref.at[p], p, z).wait_send()
        for sgn in (1, -1):
            @pl.when(inside(z + sgn))
            def _():
                to_chip(own_ref.at[p], p, z, sgn, 0).wait_send()
            for h in range(1, CHIPS):
                chip = z - sgn * h

                @pl.when(inside(chip))
                def _():
                    here = slot(p, chip, core)
                    if h < CHIPS - 1:
                        @pl.when(inside(z + sgn))
                        def _():
                            to_chip(here, p, chip, sgn, h).wait_send()
                    to_partner(here, p, chip).wait_send()
    for t in range(n):
        part_copy(t).wait_send()
    for o in range(1, n):
        pole_copy(o).wait_send()
    trace_copy.wait_send()
    for o in range(1, CHIPS):
        line_copy(wsum, wz, ss_wz, rs_wz, o).wait_send()
        line_copy(tacc, tz, ss_tz, rs_tz, o).wait_send()


def per_device(inverse_blocks, panel_blocks, ancestor_mask, diag_inverse, pole_weights, pole_order):
    local, width = panel_blocks.shape[:2]
    sn = ancestor_mask.shape[1]
    span = sn * width
    n = lax.axis_size("pole")
    rg = lax.axis_size("blk") // PC
    cw = span // n
    piece = span // (PC * rg)
    me = lax.axis_index("blk")
    mask_row = jnp.broadcast_to(ancestor_mask[0].astype(BF16)[None, :, None], (2, sn, width)).reshape(2 * span)
    own_panel = panel_blocks * mask_row[None, None, :]
    arrays = [pole_weights, pole_order, ancestor_mask, inverse_blocks, own_panel]
    if rg > 1:
        pieces = [own_panel] + [from_behind(own_panel, "blk", o * PC) for o in range(1, rg)]
        arrays.append(jnp.roll(jnp.stack(pieces[::-1], axis=1), me // PC + 1, axis=1))
    arrays.append(diag_inverse)
    smem = pl.BlockSpec(memory_space=pltpu.SMEM)
    vmem = pl.BlockSpec(memory_space=pltpu.VMEM)
    diag_shape = (piece, width // n) if rg == 1 else (rg * piece, width)
    dma = pltpu.SemaphoreType.DMA
    density, diag = pl.pallas_call(
        functools.partial(kernel, (n, rg, local, width, sn)),
        out_shape=(jax.ShapeDtypeStruct((width, cw), F32), jax.ShapeDtypeStruct(diag_shape, F32)),
        in_specs=[smem] * 3 + [vmem] * (len(arrays) - 3),
        out_specs=(vmem, vmem),
        scratch_shapes=[
            pltpu.VMEM((local, PC * width, 2 * span), BF16),
            pltpu.VMEM((local, rg * 2 * width, 2 * span), F32),
            pltpu.VMEM((n, CHIPS, 2, width, cw), F32),
            pltpu.VMEM((n, CHIPS, width, cw), F32),
            pltpu.VMEM((n, CHIPS, width, cw), F32),
            pltpu.VMEM((n - 1, CHIPS, width, cw), F32),
            pltpu.VMEM((CHIPS, width, cw), F32),
            pltpu.VMEM((CHIPS - 1, width, cw), F32),
            pltpu.VMEM((CHIPS, 2, rg, piece, width), F32),
            pltpu.VMEM((CHIPS, rg, piece, width), F32),
            pltpu.VMEM((CHIPS, rg, piece, width), F32),
            pltpu.VMEM((CHIPS - 1, rg, piece, width), F32),
            pltpu.VMEM((piece, width), F32),
            pltpu.VMEM((n - 1, piece, width), F32),
            dma((2, CHIPS - 1, local)), dma((CHIPS, local)), dma((CHIPS, local)), dma((CHIPS, local)),
            dma((n,)), dma((n,)), dma((n - 1,)), dma((n - 1,)), dma((CHIPS - 1,)), dma((CHIPS - 1,)),
            dma((1,)), dma((1,)), dma((CHIPS - 1,)), dma((CHIPS - 1,)), dma((n - 1,)), dma((n - 1,)),
        ],
        compiler_params=pltpu.CompilerParams(collective_id=0, has_side_effects=True),
    )(*arrays)
    if rg > 1:
        groups = [[r * PC + b for r in range(rg)] for b in range(PC)]
        diag = lax.psum_scatter(diag, "blk", scatter_dimension=0, axis_index_groups=groups, tiled=True)
        chosen = lax.dynamic_slice_in_dim(pole_order, lax.axis_index("pole") * local, local, 0)
        pairs = pole_weights[chosen]
        diag = diag + jnp.sum(
            pairs[:, 0, None, None] * diag_inverse[..., :width] - pairs[:, 1, None, None] * diag_inverse[..., width:],
            axis=0)
        diag = lax.psum_scatter(diag, "pole", scatter_dimension=1, tiled=True)
    return density, diag


def solution(mesh):
    placed = (
        P("pole", "blk", None),
        P("pole", "blk", None),
        P("blk", None),
        P("pole", "blk", None),
        P(),
        P(),
    )
    return jax.shard_map(
        per_device,
        mesh=mesh,
        in_specs=placed,
        out_specs=(P("blk", "pole"), P("blk", "pole")),
        check_vma=False,
    )
```

```python
import functools

import jax
import jax.numpy as jnp
from jax import lax
from jax.experimental import pallas as pl
from jax.experimental.pallas import tpu as pltpu
from jax.sharding import PartitionSpec as P

PC = 8
CHIPS = PC // 2
MESH = pl.DeviceIdType.MESH
F32 = jnp.float32
BF16 = jnp.bfloat16


def from_behind(array, axis, by):
    size = lax.axis_size(axis)
    return lax.ppermute(array, axis, [(i, (i + by) % size) for i in range(size)])


def dot00(left, right):
    return lax.dot_general(left, right, (((0,), (0,)), ((), ())), preferred_element_type=F32)


def kernel(cfg, *refs):
    n, rg, local, width, sn = cfg
    span = sn * width
    cw = span // n
    piece = span // (PC * rg)
    lean = rg == 1
    half = CHIPS // 2
    refs = list(refs)
    weight_ref, order_ref, mask_ref, inv_hbm, own_ref = refs[:5]
    refs = refs[5:]
    col_ref = refs.pop(0) if rg > 1 else None
    diag_ref, dens_ref, dout_ref = refs[:3]
    (inv_ref, inv_sem, far, far_gram, ss_far, rs_far, lall, gram, wfull, wrecv, wacc, wpole, wsum, wz, tbuf, trecv, tacc, tz, tsum, tpole,
     ss_z, ss_p, rs_z, rs_p, ss_wp, rs_wp, ss_wq, rs_wq, ss_wz, rs_wz,
     ss_tp, rs_tp, ss_tz, rs_tz, ss_tq, rs_tq) = refs[3:]

    me = lax.axis_index("blk")
    q = lax.axis_index("pole")
    rank = lax.rem(me, PC)
    first = me - rank
    z = rank // 2
    core = lax.rem(rank, 2)
    other = 1 - core

    def device(chip, which, pole):
        return {"pole": pole, "blk": first + 2 * chip + which}

    partner = device(z, other, q)

    def remote(src, dst, send, recv, where):
        return pltpu.make_async_remote_copy(
            src_ref=src, dst_ref=dst, send_sem=send, recv_sem=recv,
            device_id=where, device_id_type=MESH)

    peers = [partner]
    peers += [device(lax.rem(z + o, CHIPS), core, q) for o in range(1, CHIPS)]
    peers += [device(z, core, lax.rem(q + o, n)) for o in range(1, n)]
    barrier = pltpu.get_barrier_semaphore()
    for peer in peers:
        pl.semaphore_signal(barrier, inc=1, device_id=peer, device_id_type=MESH)
    inv_copy = pltpu.make_async_copy(inv_hbm, inv_ref, inv_sem.at[0])
    inv_copy.start()
    here_rows = pl.ds(pl.multiple_of(rank * width, width), width)
    for p in range(local):
        for t in range(2):
            for k in range(sn):
                at = slice((t * sn + k) * width, (t * sn + k + 1) * width)
                value = own_ref[p, :, at]
                if lean:
                    value = (value.astype(F32) * mask_ref[0, k].astype(F32)).astype(BF16)
                lall[p, here_rows, at] = value
    pl.semaphore_wait(barrier, len(peers))

    def slot(p, chip, which):
        return lall.at[p, pl.ds(pl.multiple_of((2 * chip + which) * width, width), width)]

    def to_chip(src, p, chip, sgn, h):
        return remote(src, slot(p, chip, core), ss_z.at[(1 - sgn) // 2, h, p], rs_z.at[chip, p],
                      device(z + sgn, core, q))

    def to_partner(src, p, chip):
        return remote(src, slot(p, chip, core), ss_p.at[chip, p], rs_p.at[chip, p], partner)

    def inside(chip):
        return jnp.logical_and(chip >= 0, chip < CHIPS)

    for p in range(local):
        for sgn in (1, -1):
            @pl.when(inside(z + sgn))
            def _():
                to_chip(slot(p, z, core), p, z, sgn, 0).start()
    for p in range(local):
        to_partner(slot(p, z, core), p, z).start()
    inv_copy.wait()

    def far_copy(p, chip):
        to, rows = (1, half * 2 * width) if chip == 0 else (CHIPS - 2, 0)
        return remote(inv_ref.at[p, pl.ds(rows, half * 2 * width)], far.at[p], ss_far.at[p], rs_far.at[p],
                      device(to, core, q))

    if lean:
        for chip in (0, CHIPS - 1):
            @pl.when(z == chip)
            def _():
                for p in range(local):
                    far_copy(p, chip).start()

    poles = [order_ref[q * local + p] for p in range(local)]
    w_re = [weight_ref[0, poles[p]] for p in range(local)]
    w_im = [weight_ref[1, poles[p]] for p in range(local)]

    def column(p, a):
        return slot(p, z, core) if lean else col_ref.at[p, a]

    def part_copy(t):
        return remote(wfull.at[t, :, other], wrecv.at[t], ss_wp.at[t], rs_wp.at[t], partner)

    order = [lax.rem(q + o, n) for o in list(range(1, n)) + [0]]
    for t in order:
        total = None
        for p in range(local):
            product = None
            for a in range(rg):
                block = column(p, a)
                re = block[:, pl.ds(pl.multiple_of(t * cw, 128), cw)]
                im = block[:, pl.ds(pl.multiple_of(span + t * cw, 128), cw)]
                real_form = jnp.concatenate(
                    [jnp.concatenate([re, im], axis=1), jnp.concatenate([-im, re], axis=1)], axis=0)
                term = jnp.dot(inv_ref[p, :, 2 * width * a:2 * width * (a + 1)], real_form,
                               preferred_element_type=F32)
                product = term if product is None else product + term
            term = w_im[p] * product[:, cw:] - w_re[p] * product[:, :cw]
            total = term if total is None else total + term
        wfull[t] = total.reshape(CHIPS, 2, width, cw)
        part_copy(t).start()

    def middle(chip):
        return jnp.logical_and(chip >= 1, chip < CHIPS - 1)

    def takes(chip, h):
        if lean and h > 1:
            return jnp.logical_and(inside(chip), middle(z)) if h == 2 else False
        return inside(chip)

    def passes_on(sgn, h):
        if lean:
            return middle(z + sgn) if h == 1 else False
        return inside(z + sgn) if h < CHIPS - 1 else False

    def hop(h):
        for p in range(local):
            for sgn in (1, -1):
                chip = z - sgn * h

                @pl.when(takes(chip, h))
                def _():
                    here = slot(p, chip, core)
                    remote(here, here, ss_p.at[chip, p], rs_z.at[chip, p], partner).wait_recv()
                    if passes_on(sgn, h) is not False:
                        @pl.when(passes_on(sgn, h))
                        def _():
                            to_chip(here, p, chip, sgn, h).start()
                    to_partner(here, p, chip).start()

    def accumulate(chip, fresh):
        rows = pl.ds(pl.multiple_of(chip * 2 * width, 2 * width), 2 * width)
        for p in range(local):
            theirs = slot(p, chip, other)
            remote(theirs, theirs, ss_p.at[chip, p], rs_p.at[chip, p], partner).wait_recv()
            for a in range(rg):
                at = slice(2 * width * a, 2 * width * (a + 1))
                term = dot00(inv_ref[p, rows, at], lall[p, rows, :])
                gram[p, at, :] = term if fresh else gram[p, at, :] + term

    def gather(h):
        for sgn in (1, -1):
            chip = z - sgn * h

            @pl.when(takes(chip, h))
            def _():
                accumulate(chip, False)

    def pole_copy(o):
        to = lax.rem(q + o, n)
        return remote(wacc.at[to], wpole.at[o - 1], ss_wq.at[o - 1], rs_wq.at[o - 1], device(z, core, to))

    def line_copy(src, dst, send, recv, o):
        to = lax.rem(z + o, CHIPS)
        return remote(src.at[to], dst.at[o - 1], send.at[o - 1], recv.at[o - 1], device(to, core, q))

    hop(1)
    for o in list(range(1, n)) + [0]:
        t = lax.rem(q + o, n)
        part_copy(t).wait_recv()
        wacc[t] = wfull[t, :, core] + wrecv[t]
        if o:
            pole_copy(o).start()
    accumulate(z, True)
    gather(1)
    hop(2)
    for o in range(1, n):
        pole_copy(o).wait_recv()
    wsum[...] = wacc[q] + functools.reduce(lambda x, y: x + y, [wpole[o] for o in range(n - 1)])
    for o in range(1, CHIPS):
        line_copy(wsum, wz, ss_wz, rs_wz, o).start()
    gather(2)
    if not lean:
        hop(3)
        gather(3)
    else:
        for near in (1, CHIPS - 2):
            @pl.when(z == near)
            def _():
                end, base = (0, half) if near == 1 else (CHIPS - 1, 0)
                rows = pl.ds(base * 2 * width, half * 2 * width)
                for p in range(local):
                    far_copy(p, end).wait_recv()
                    far_gram[p] = dot00(far[p], lall[p, rows, :])

    per_width = width // piece

    def add_traces(traces, p, upper, lower, block):
        m_re = upper[:, :span] - lower[:, span:]
        m_im = lower[:, :span] + upper[:, span:]
        n_re = w_re[p] * m_re - w_im[p] * m_im
        n_im = w_re[p] * m_im + w_im[p] * m_re
        both = jnp.concatenate([n_re, -n_im], axis=0)
        high = both.astype(BF16)
        low = (both - high.astype(F32)).astype(BF16)
        for k in range(sn):
            at = slice(k * width, (k + 1) * width)
            right = jnp.concatenate([block[:, at], block[:, span + k * width:span + (k + 1) * width]], axis=0)
            term = dot00(high[:, at], right) + dot00(low[:, at], right)
            traces[k] = term if traces[k] is None else traces[k] + term

    traces = [None] * sn
    for p in range(local):
        for a in range(rg):
            base = 2 * width * a
            add_traces(traces, p, gram[p, base:base + width, :], gram[p, base + width:base + 2 * width, :],
                       column(p, a))
    for g in range(PC * rg):
        k, off = g // per_width, g % per_width * piece
        tbuf[g % PC // 2, g % 2, g // PC] = traces[k][off:off + piece]
    if lean:
        @pl.when(middle(z))
        def _():
            more = [None] * sn
            for p in range(local):
                add_traces(more, p, far_gram[p, :width, :], far_gram[p, width:, :],
                           slot(p, (z - 1) * (CHIPS - 1), core))
            for g in range(PC):
                k, off = g // per_width, g % per_width * piece
                tbuf[g // 2, g % 2, 0] += more[k][off:off + piece]
    trace_copy = remote(tbuf.at[:, other], trecv, ss_tp.at[0], rs_tp.at[0], partner)
    trace_copy.start()

    for o in range(1, CHIPS):
        line_copy(wsum, wz, ss_wz, rs_wz, o).wait_recv()
    rows = wsum[z] + functools.reduce(lambda x, y: x + y, [wz[o] for o in range(CHIPS - 1)])
    for j in range(cw // width):
        at = slice(j * width, (j + 1) * width)
        dens_ref[:, at] = rows[:, at] * mask_ref[0, q * (cw // width) + j].astype(F32)

    trace_copy.wait_recv()
    tacc[...] = tbuf[:, core] + trecv[...]
    for o in range(1, CHIPS):
        line_copy(tacc, tz, ss_tz, rs_tz, o).start()
    for o in range(1, CHIPS):
        line_copy(tacc, tz, ss_tz, rs_tz, o).wait_recv()
    summed = tacc[z] + functools.reduce(lambda x, y: x + y, [tz[o] for o in range(CHIPS - 1)])
    if rg > 1:
        dout_ref[...] = summed.reshape(rg * piece, width)
    else:
        summed = summed.reshape(piece, width)
        for p in range(local):
            summed = summed + w_re[p] * diag_ref[p, :, :width] - w_im[p] * diag_ref[p, :, width:]
        tsum[...] = summed

        def last_copy(o):
            return remote(tsum, tpole.at[o - 1], ss_tq.at[o - 1], rs_tq.at[o - 1],
                          device(z, core, lax.rem(q + o, n)))

        for o in range(1, n):
            last_copy(o).start()
        for o in range(1, n):
            last_copy(o).wait_recv()
        summed = summed + functools.reduce(lambda x, y: x + y, [tpole[o] for o in range(n - 1)])
        narrow = width // n
        summed = summed.T
        result = jnp.zeros((narrow, piece), F32)
        for t in range(n):
            result = jnp.where(q == t, summed[t * narrow:(t + 1) * narrow], result)
        dout_ref[...] = result
        for o in range(1, n):
            last_copy(o).wait_send()

    for p in range(local):
        to_partner(slot(p, z, core), p, z).wait_send()
        for sgn in (1, -1):
            @pl.when(inside(z + sgn))
            def _():
                to_chip(slot(p, z, core), p, z, sgn, 0).wait_send()
            for h in range(1, half + 1 if lean else CHIPS):
                chip = z - sgn * h

                @pl.when(takes(chip, h))
                def _():
                    here = slot(p, chip, core)
                    if passes_on(sgn, h) is not False:
                        @pl.when(passes_on(sgn, h))
                        def _():
                            to_chip(here, p, chip, sgn, h).wait_send()
                    to_partner(here, p, chip).wait_send()
    if lean:
        for chip in (0, CHIPS - 1):
            @pl.when(z == chip)
            def _():
                for p in range(local):
                    far_copy(p, chip).wait_send()
    for t in range(n):
        part_copy(t).wait_send()
    for o in range(1, n):
        pole_copy(o).wait_send()
    trace_copy.wait_send()
    for o in range(1, CHIPS):
        line_copy(wsum, wz, ss_wz, rs_wz, o).wait_send()
        line_copy(tacc, tz, ss_tz, rs_tz, o).wait_send()


def per_device(inverse_blocks, panel_blocks, ancestor_mask, diag_inverse, pole_weights, pole_order):
    local, width = panel_blocks.shape[:2]
    sn = ancestor_mask.shape[1]
    span = sn * width
    n = lax.axis_size("pole")
    rg = lax.axis_size("blk") // PC
    cw = span // n
    piece = span // (PC * rg)
    me = lax.axis_index("blk")
    mask_row = jnp.broadcast_to(ancestor_mask[0].astype(BF16)[None, :, None], (2, sn, width)).reshape(2 * span)
    own_panel = panel_blocks * mask_row[None, None, :] if rg > 1 else panel_blocks
    arrays = [pole_weights.T, pole_order, ancestor_mask, inverse_blocks, own_panel]
    if rg > 1:
        pieces = [own_panel] + [from_behind(own_panel, "blk", o * PC) for o in range(1, rg)]
        arrays.append(jnp.roll(jnp.stack(pieces[::-1], axis=1), me // PC + 1, axis=1))
    arrays.append(diag_inverse)
    smem = pl.BlockSpec(memory_space=pltpu.SMEM)
    vmem = pl.BlockSpec(memory_space=pltpu.VMEM)
    diag_shape = (width // n, piece) if rg == 1 else (rg * piece, width)
    dma = pltpu.SemaphoreType.DMA
    density, diag = pl.pallas_call(
        functools.partial(kernel, (n, rg, local, width, sn)),
        out_shape=(jax.ShapeDtypeStruct((width, cw), F32), jax.ShapeDtypeStruct(diag_shape, F32)),
        in_specs=[smem] * 3 + [pl.BlockSpec(memory_space=pl.ANY)] + [vmem] * (len(arrays) - 4),
        out_specs=(vmem, vmem),
        scratch_shapes=[
            pltpu.VMEM(inverse_blocks.shape, BF16), dma((1,)),
            pltpu.VMEM((local, CHIPS // 2 * 2 * width, 2 * width) if rg == 1 else (8, 128), BF16),
            pltpu.VMEM((local, 2 * width, 2 * span) if rg == 1 else (8, 128), F32),
            dma((local,)), dma((local,)),
            pltpu.VMEM((local, PC * width, 2 * span), BF16),
            pltpu.VMEM((local, rg * 2 * width, 2 * span), F32),
            pltpu.VMEM((n, CHIPS, 2, width, cw), F32),
            pltpu.VMEM((n, CHIPS, width, cw), F32),
            pltpu.VMEM((n, CHIPS, width, cw), F32),
            pltpu.VMEM((n - 1, CHIPS, width, cw), F32),
            pltpu.VMEM((CHIPS, width, cw), F32),
            pltpu.VMEM((CHIPS - 1, width, cw), F32),
            pltpu.VMEM((CHIPS, 2, rg, piece, width), F32),
            pltpu.VMEM((CHIPS, rg, piece, width), F32),
            pltpu.VMEM((CHIPS, rg, piece, width), F32),
            pltpu.VMEM((CHIPS - 1, rg, piece, width), F32),
            pltpu.VMEM((piece, width), F32),
            pltpu.VMEM((n - 1, piece, width), F32),
            dma((2, CHIPS - 1, local)), dma((CHIPS, local)), dma((CHIPS, local)), dma((CHIPS, local)),
            dma((n,)), dma((n,)), dma((n - 1,)), dma((n - 1,)), dma((CHIPS - 1,)), dma((CHIPS - 1,)),
            dma((1,)), dma((1,)), dma((CHIPS - 1,)), dma((CHIPS - 1,)), dma((n - 1,)), dma((n - 1,)),
        ],
        compiler_params=pltpu.CompilerParams(collective_id=0, has_side_effects=True),
    )(*arrays)
    if rg > 1:
        groups = [[r * PC + b for r in range(rg)] for b in range(PC)]
        diag = lax.psum_scatter(diag, "blk", scatter_dimension=0, axis_index_groups=groups, tiled=True)
        chosen = lax.dynamic_slice_in_dim(pole_order, lax.axis_index("pole") * local, local, 0)
        pairs = pole_weights[chosen]
        diag = diag + jnp.sum(
            pairs[:, 0, None, None] * diag_inverse[..., :width] - pairs[:, 1, None, None] * diag_inverse[..., width:],
            axis=0)
        diag = lax.psum_scatter(diag, "pole", scatter_dimension=1, tiled=True)
    else:
        diag = diag.T
    return density, diag


def solution(mesh):
    placed = (
        P("pole", "blk", None),
        P("pole", "blk", None),
        P("blk", None),
        P("pole", "blk", None),
        P(),
        P(),
    )
    return jax.shard_map(
        per_device,
        mesh=mesh,
        in_specs=placed,
        out_specs=(P("blk", "pole"), P("blk", "pole")),
        check_vma=False,
    )
```

```python
import functools

import jax
import jax.numpy as jnp
from jax import lax
from jax.experimental import pallas as pl
from jax.experimental.pallas import tpu as pltpu
from jax.sharding import PartitionSpec as P

PC = 8
CHIPS = PC // 2
MESH = pl.DeviceIdType.MESH
F32 = jnp.float32
BF16 = jnp.bfloat16


def from_behind(array, axis, by):
    size = lax.axis_size(axis)
    return lax.ppermute(array, axis, [(i, (i + by) % size) for i in range(size)])


def dot00(left, right):
    return lax.dot_general(left, right, (((0,), (0,)), ((), ())), preferred_element_type=F32)


def kernel(cfg, *refs):
    n, rg, local, width, sn = cfg
    span = sn * width
    cw = span // n
    piece = span // (PC * rg)
    lean = rg == 1
    half = CHIPS // 2
    refs = list(refs)
    weight_ref, order_ref, mask_ref, inv_hbm, own_ref = refs[:5]
    refs = refs[5:]
    col_ref = refs.pop(0) if rg > 1 else None
    diag_ref, dens_ref, dout_ref = refs[:3]
    (inv_ref, inv_sem, far, far_gram, tt, ss_far, rs_far, lall, gram, wfull, wrecv, wacc, wpole, wsum, wz, tbuf, trecv, tacc, tz, tsum, tpole,
     ss_z, ss_p, rs_z, rs_p, ss_wp, rs_wp, ss_wq, rs_wq, ss_wz, rs_wz,
     ss_tp, rs_tp, ss_tz, rs_tz, ss_tq, rs_tq) = refs[3:]

    me = lax.axis_index("blk")
    q = lax.axis_index("pole")
    rank = lax.rem(me, PC)
    first = me - rank
    z = rank // 2
    core = lax.rem(rank, 2)
    other = 1 - core

    def device(chip, which, pole):
        return {"pole": pole, "blk": first + 2 * chip + which}

    partner = device(z, other, q)

    def remote(src, dst, send, recv, where):
        return pltpu.make_async_remote_copy(
            src_ref=src, dst_ref=dst, send_sem=send, recv_sem=recv,
            device_id=where, device_id_type=MESH)

    peers = [partner]
    peers += [device(lax.rem(z + o, CHIPS), core, q) for o in range(1, CHIPS)]
    peers += [device(z, core, lax.rem(q + o, n)) for o in range(1, n)]
    barrier = pltpu.get_barrier_semaphore()
    for peer in peers:
        pl.semaphore_signal(barrier, inc=1, device_id=peer, device_id_type=MESH)
    inv_copy = pltpu.make_async_copy(inv_hbm, inv_ref, inv_sem.at[0])
    inv_copy.start()
    here_rows = pl.ds(pl.multiple_of(rank * width, width), width)
    for p in range(local):
        for t in range(2):
            for k in range(sn):
                at = slice((t * sn + k) * width, (t * sn + k + 1) * width)
                value = own_ref[p, :, at]
                if lean:
                    value = (value.astype(F32) * mask_ref[0, k].astype(F32)).astype(BF16)
                lall[p, here_rows, at] = value
    pl.semaphore_wait(barrier, len(peers))

    def slot(p, chip, which):
        return lall.at[p, pl.ds(pl.multiple_of((2 * chip + which) * width, width), width)]

    def to_chip(src, p, chip, sgn, h):
        return remote(src, slot(p, chip, core), ss_z.at[(1 - sgn) // 2, h, p], rs_z.at[chip, p],
                      device(z + sgn, core, q))

    def to_partner(src, p, chip):
        return remote(src, slot(p, chip, core), ss_p.at[chip, p], rs_p.at[chip, p], partner)

    def inside(chip):
        return jnp.logical_and(chip >= 0, chip < CHIPS)

    for p in range(local):
        for sgn in (1, -1):
            @pl.when(inside(z + sgn))
            def _():
                to_chip(slot(p, z, core), p, z, sgn, 0).start()
    for p in range(local):
        to_partner(slot(p, z, core), p, z).start()
    inv_copy.wait()

    def far_copy(p, chip):
        to, rows = (1, half * 2 * width) if chip == 0 else (CHIPS - 2, 0)
        return remote(inv_ref.at[p, pl.ds(rows, half * 2 * width)], far.at[p], ss_far.at[p], rs_far.at[p],
                      device(to, core, q))

    if lean:
        for chip in (0, CHIPS - 1):
            @pl.when(z == chip)
            def _():
                for p in range(local):
                    far_copy(p, chip).start()

    poles = [order_ref[q * local + p] for p in range(local)]
    w_re = [weight_ref[0, poles[p]] for p in range(local)]
    w_im = [weight_ref[1, poles[p]] for p in range(local)]

    def column(p, a):
        return slot(p, z, core) if lean else col_ref.at[p, a]

    def part_copy(t):
        return remote(wfull.at[t, :, other], wrecv.at[t], ss_wp.at[t], rs_wp.at[t], partner)

    order = [lax.rem(q + o, n) for o in list(range(1, n)) + [0]]
    for t in order:
        total = None
        for p in range(local):
            product = None
            for a in range(rg):
                block = column(p, a)
                re = block[:, pl.ds(pl.multiple_of(t * cw, 128), cw)]
                im = block[:, pl.ds(pl.multiple_of(span + t * cw, 128), cw)]
                real_form = jnp.concatenate(
                    [jnp.concatenate([re, im], axis=1), jnp.concatenate([-im, re], axis=1)], axis=0)
                term = jnp.dot(inv_ref[p, :, 2 * width * a:2 * width * (a + 1)], real_form,
                               preferred_element_type=F32)
                product = term if product is None else product + term
            term = w_im[p] * product[:, cw:] - w_re[p] * product[:, :cw]
            total = term if total is None else total + term
        wfull[t] = total.reshape(CHIPS, 2, width, cw)
        part_copy(t).start()

    def middle(chip):
        return jnp.logical_and(chip >= 1, chip < CHIPS - 1)

    def takes(chip, h):
        if lean and h > 1:
            return jnp.logical_and(inside(chip), middle(z)) if h == 2 else False
        return inside(chip)

    def passes_on(sgn, h):
        if lean:
            return middle(z + sgn) if h == 1 else False
        return inside(z + sgn) if h < CHIPS - 1 else False

    every = range(local)

    def hop(h, ps=every):
        for p in ps:
            for sgn in (1, -1):
                chip = z - sgn * h

                @pl.when(takes(chip, h))
                def _():
                    here = slot(p, chip, core)
                    remote(here, here, ss_p.at[chip, p], rs_z.at[chip, p], partner).wait_recv()
                    if passes_on(sgn, h) is not False:
                        @pl.when(passes_on(sgn, h))
                        def _():
                            to_chip(here, p, chip, sgn, h).start()
                    to_partner(here, p, chip).start()

    def accumulate(chip, fresh, ps=every):
        rows = pl.ds(pl.multiple_of(chip * 2 * width, 2 * width), 2 * width)
        for p in ps:
            theirs = slot(p, chip, other)
            remote(theirs, theirs, ss_p.at[chip, p], rs_p.at[chip, p], partner).wait_recv()
            for a in range(rg):
                at = slice(2 * width * a, 2 * width * (a + 1))
                term = dot00(inv_ref[p, rows, at], lall[p, rows, :])
                gram[p, at, :] = term if fresh else gram[p, at, :] + term

    def gather(h, ps=every):
        for sgn in (1, -1):
            chip = z - sgn * h

            @pl.when(takes(chip, h))
            def _():
                accumulate(chip, False, ps)

    def pole_copy(o):
        to = lax.rem(q + o, n)
        return remote(wacc.at[to], wpole.at[o - 1], ss_wq.at[o - 1], rs_wq.at[o - 1], device(z, core, to))

    def line_copy(src, dst, send, recv, o):
        to = lax.rem(z + o, CHIPS)
        return remote(src.at[to], dst.at[o - 1], send.at[o - 1], recv.at[o - 1], device(to, core, q))

    hop(1)
    for o in list(range(1, n)) + [0]:
        t = lax.rem(q + o, n)
        part_copy(t).wait_recv()
        wacc[t] = wfull[t, :, core] + wrecv[t]
        if o:
            pole_copy(o).start()
    accumulate(z, True)
    gather(1)

    per_width = width // piece

    def add_traces(fresh, p, upper, lower, block):
        m_re = upper[:, :span] - lower[:, span:]
        m_im = lower[:, :span] + upper[:, span:]
        n_re = w_re[p] * m_re - w_im[p] * m_im
        n_im = w_re[p] * m_im + w_im[p] * m_re
        both = jnp.concatenate([n_re, -n_im], axis=0)
        high = both.astype(BF16)
        low = (both - high.astype(F32)).astype(BF16)
        for k in range(sn):
            at = slice(k * width, (k + 1) * width)
            left = jnp.concatenate([block[:, at], block[:, span + k * width:span + (k + 1) * width]], axis=0)
            term = dot00(left, jnp.concatenate([high[:, at], low[:, at]], axis=1))
            term = term[:, :width] + term[:, width:]
            tt[k] = term if fresh else tt[k] + term

    def own_traces(p):
        for a in range(rg):
            base = 2 * width * a
            add_traces(p == 0 and a == 0, p, gram[p, base:base + width, :],
                       gram[p, base + width:base + 2 * width, :], column(p, a))

    def reduce_density():
        for o in range(1, n):
            pole_copy(o).wait_recv()
        wsum[...] = wacc[q] + functools.reduce(lambda x, y: x + y, [wpole[o] for o in range(n - 1)])
        for o in range(1, CHIPS):
            line_copy(wsum, wz, ss_wz, rs_wz, o).start()

    if lean:
        for p in range(local):
            hop(2, [p])
            gather(2, [p])
            own_traces(p)
            for near in (1, CHIPS - 2):
                @pl.when(z == near)
                def _():
                    end, base = (0, half) if near == 1 else (CHIPS - 1, 0)
                    rows = slice(base * 2 * width, (base + half) * 2 * width)
                    far_copy(p, end).wait_recv()
                    far_gram[p] = dot00(far[p], lall[p, rows, :])
                    add_traces(False, p, far_gram[p, :width, :], far_gram[p, width:, :], slot(p, end, core))
            if p == 0:
                reduce_density()
    else:
        hop(2)
        reduce_density()
        gather(2)
        hop(3)
        gather(3)
        for p in range(local):
            own_traces(p)
    for k in range(sn):
        trace = tt[k].T
        for g in range(k * per_width, (k + 1) * per_width):
            off = g % per_width * piece
            tbuf[g % PC // 2, g % 2, g // PC] = trace[off:off + piece]
    trace_copy = remote(tbuf.at[:, other], trecv, ss_tp.at[0], rs_tp.at[0], partner)
    trace_copy.start()

    for o in range(1, CHIPS):
        line_copy(wsum, wz, ss_wz, rs_wz, o).wait_recv()
    rows = wsum[z] + functools.reduce(lambda x, y: x + y, [wz[o] for o in range(CHIPS - 1)])
    for j in range(cw // width):
        at = slice(j * width, (j + 1) * width)
        dens_ref[:, at] = rows[:, at] * mask_ref[0, q * (cw // width) + j].astype(F32)

    trace_copy.wait_recv()
    tacc[...] = tbuf[:, core] + trecv[...]
    for o in range(1, CHIPS):
        line_copy(tacc, tz, ss_tz, rs_tz, o).start()
    for o in range(1, CHIPS):
        line_copy(tacc, tz, ss_tz, rs_tz, o).wait_recv()
    summed = tacc[z] + functools.reduce(lambda x, y: x + y, [tz[o] for o in range(CHIPS - 1)])
    if rg > 1:
        dout_ref[...] = summed.reshape(rg * piece, width)
    else:
        summed = summed.reshape(piece, width)
        for p in range(local):
            summed = summed + w_re[p] * diag_ref[p, :, :width] - w_im[p] * diag_ref[p, :, width:]
        narrow = width // n
        summed = summed.T
        for t in range(n):
            tsum[t] = summed[t * narrow:(t + 1) * narrow]

        def last_copy(o):
            to = lax.rem(q + o, n)
            return remote(tsum.at[to], tpole.at[o - 1], ss_tq.at[o - 1], rs_tq.at[o - 1], device(z, core, to))

        for o in range(1, n):
            last_copy(o).start()
        for o in range(1, n):
            last_copy(o).wait_recv()
        dout_ref[...] = tsum[q] + functools.reduce(lambda x, y: x + y, [tpole[o] for o in range(n - 1)])
        for o in range(1, n):
            last_copy(o).wait_send()

    for p in range(local):
        to_partner(slot(p, z, core), p, z).wait_send()
        for sgn in (1, -1):
            @pl.when(inside(z + sgn))
            def _():
                to_chip(slot(p, z, core), p, z, sgn, 0).wait_send()
            for h in range(1, half + 1 if lean else CHIPS):
                chip = z - sgn * h

                @pl.when(takes(chip, h))
                def _():
                    here = slot(p, chip, core)
                    if passes_on(sgn, h) is not False:
                        @pl.when(passes_on(sgn, h))
                        def _():
                            to_chip(here, p, chip, sgn, h).wait_send()
                    to_partner(here, p, chip).wait_send()
    if lean:
        for chip in (0, CHIPS - 1):
            @pl.when(z == chip)
            def _():
                for p in range(local):
                    far_copy(p, chip).wait_send()
    for t in range(n):
        part_copy(t).wait_send()
    for o in range(1, n):
        pole_copy(o).wait_send()
    trace_copy.wait_send()
    for o in range(1, CHIPS):
        line_copy(wsum, wz, ss_wz, rs_wz, o).wait_send()
        line_copy(tacc, tz, ss_tz, rs_tz, o).wait_send()


def land(*arrays):
    def move(*refs):
        for source, target in zip(refs[:len(arrays)], refs[len(arrays):]):
            target[...] = source[...]

    return pl.pallas_call(move, out_shape=[jax.ShapeDtypeStruct(x.shape, x.dtype) for x in arrays])(*arrays)


def per_device(inverse_blocks, panel_blocks, ancestor_mask, diag_inverse, pole_weights, pole_order):
    local, width = panel_blocks.shape[:2]
    sn = ancestor_mask.shape[1]
    span = sn * width
    n = lax.axis_size("pole")
    rg = lax.axis_size("blk") // PC
    cw = span // n
    piece = span // (PC * rg)
    me = lax.axis_index("blk")
    mask_row = jnp.broadcast_to(ancestor_mask[0].astype(BF16)[None, :, None], (2, sn, width)).reshape(2 * span)
    own_panel = panel_blocks * mask_row[None, None, :] if rg > 1 else panel_blocks
    arrays = [pole_weights.T, pole_order, ancestor_mask, inverse_blocks, own_panel]
    if rg > 1:
        pieces = [own_panel] + [from_behind(own_panel, "blk", o * PC) for o in range(1, rg)]
        arrays.append(jnp.roll(jnp.stack(pieces[::-1], axis=1), me // PC + 1, axis=1))
    arrays.append(diag_inverse)
    smem = pl.BlockSpec(memory_space=pltpu.SMEM)
    vmem = pl.BlockSpec(memory_space=pltpu.VMEM)
    diag_shape = (width // n, piece) if rg == 1 else (rg * piece, width)
    dma = pltpu.SemaphoreType.DMA
    density, diag = pl.pallas_call(
        functools.partial(kernel, (n, rg, local, width, sn)),
        out_shape=(jax.ShapeDtypeStruct((width, cw), F32), jax.ShapeDtypeStruct(diag_shape, F32)),
        in_specs=[smem] * 3 + [pl.BlockSpec(memory_space=pl.ANY)] + [vmem] * (len(arrays) - 4),
        out_specs=(vmem, vmem),
        scratch_shapes=[
            pltpu.VMEM(inverse_blocks.shape, BF16), dma((1,)),
            pltpu.VMEM((local, CHIPS // 2 * 2 * width, 2 * width) if rg == 1 else (8, 128), BF16),
            pltpu.VMEM((local, 2 * width, 2 * span) if rg == 1 else (8, 128), F32),
            pltpu.VMEM((sn, width, width), F32),
            dma((local,)), dma((local,)),
            pltpu.VMEM((local, PC * width, 2 * span), BF16),
            pltpu.VMEM((local, rg * 2 * width, 2 * span), F32),
            pltpu.VMEM((n, CHIPS, 2, width, cw), F32),
            pltpu.VMEM((n, CHIPS, width, cw), F32),
            pltpu.VMEM((n, CHIPS, width, cw), F32),
            pltpu.VMEM((n - 1, CHIPS, width, cw), F32),
            pltpu.VMEM((CHIPS, width, cw), F32),
            pltpu.VMEM((CHIPS - 1, width, cw), F32),
            pltpu.VMEM((CHIPS, 2, rg, piece, width), F32),
            pltpu.VMEM((CHIPS, rg, piece, width), F32),
            pltpu.VMEM((CHIPS, rg, piece, width), F32),
            pltpu.VMEM((CHIPS - 1, rg, piece, width), F32),
            pltpu.VMEM((n, width // n, piece), F32),
            pltpu.VMEM((n - 1, width // n, piece), F32),
            dma((2, CHIPS - 1, local)), dma((CHIPS, local)), dma((CHIPS, local)), dma((CHIPS, local)),
            dma((n,)), dma((n,)), dma((n - 1,)), dma((n - 1,)), dma((CHIPS - 1,)), dma((CHIPS - 1,)),
            dma((1,)), dma((1,)), dma((CHIPS - 1,)), dma((CHIPS - 1,)), dma((n - 1,)), dma((n - 1,)),
        ],
        compiler_params=pltpu.CompilerParams(collective_id=0, has_side_effects=True),
    )(*arrays)
    if rg > 1:
        groups = [[r * PC + b for r in range(rg)] for b in range(PC)]
        diag = lax.psum_scatter(diag, "blk", scatter_dimension=0, axis_index_groups=groups, tiled=True)
        chosen = lax.dynamic_slice_in_dim(pole_order, lax.axis_index("pole") * local, local, 0)
        pairs = pole_weights[chosen]
        diag = diag + jnp.sum(
            pairs[:, 0, None, None] * diag_inverse[..., :width] - pairs[:, 1, None, None] * diag_inverse[..., width:],
            axis=0)
        diag = lax.psum_scatter(diag, "pole", scatter_dimension=1, tiled=True)
    else:
        density, diag = land(density, diag)
        diag = diag.T
    return density, diag


def solution(mesh):
    placed = (
        P("pole", "blk", None),
        P("pole", "blk", None),
        P("blk", None),
        P("pole", "blk", None),
        P(),
        P(),
    )
    return jax.shard_map(
        per_device,
        mesh=mesh,
        in_specs=placed,
        out_specs=(P("blk", "pole"), P("blk", "pole")),
        check_vma=False,
    )
```

```python
import functools

import jax
import jax.numpy as jnp
from jax import lax
from jax.experimental import pallas as pl
from jax.experimental.pallas import tpu as pltpu
from jax.sharding import PartitionSpec as P

PC = 8
CHIPS = PC // 2
MESH = pl.DeviceIdType.MESH
F32 = jnp.float32
BF16 = jnp.bfloat16


def from_behind(array, axis, by):
    size = lax.axis_size(axis)
    return lax.ppermute(array, axis, [(i, (i + by) % size) for i in range(size)])


def dot00(left, right):
    return lax.dot_general(left, right, (((0,), (0,)), ((), ())), preferred_element_type=F32)


def kernel(cfg, *refs):
    n, rg, local, width, sn = cfg
    span = sn * width
    cw = span // n
    piece = span // (PC * rg)
    lean = rg == 1
    half = CHIPS // 2
    refs = list(refs)
    weight_ref, order_ref, mask_ref, inv_hbm, own_ref = refs[:5]
    refs = refs[5:]
    col_ref = refs.pop(0) if rg > 1 else None
    diag_ref, dens_ref, dout_ref = refs[:3]
    (inv_ref, inv_sem, far, far_gram, tt, ss_far, rs_far, lall, gram, wfull, wrecv, wacc, wpole, wsum, wz, tbuf, trecv, tacc, tz, tsum, tpole,
     ss_z, ss_p, rs_z, rs_p, ss_wp, rs_wp, ss_wq, rs_wq, ss_wz, rs_wz,
     ss_tp, rs_tp, ss_tz, rs_tz, ss_tq, rs_tq) = refs[3:]

    me = lax.axis_index("blk")
    q = lax.axis_index("pole")
    rank = lax.rem(me, PC)
    first = me - rank
    z = rank // 2
    core = lax.rem(rank, 2)
    other = 1 - core

    def device(chip, which, pole):
        return {"pole": pole, "blk": first + 2 * chip + which}

    partner = device(z, other, q)

    def remote(src, dst, send, recv, where):
        return pltpu.make_async_remote_copy(
            src_ref=src, dst_ref=dst, send_sem=send, recv_sem=recv,
            device_id=where, device_id_type=MESH)

    peers = [partner]
    peers += [device(lax.rem(z + o, CHIPS), core, q) for o in range(1, CHIPS)]
    peers += [device(z, core, lax.rem(q + o, n)) for o in range(1, n)]
    barrier = pltpu.get_barrier_semaphore()
    for peer in peers:
        pl.semaphore_signal(barrier, inc=1, device_id=peer, device_id_type=MESH)
    inv_copy = pltpu.make_async_copy(inv_hbm, inv_ref, inv_sem.at[0])
    inv_copy.start()
    here_rows = pl.ds(pl.multiple_of(rank * width, width), width)
    for p in range(local):
        for t in range(2):
            for k in range(sn):
                at = slice((t * sn + k) * width, (t * sn + k + 1) * width)
                value = own_ref[p, :, at]
                if lean:
                    value = (value.astype(F32) * mask_ref[0, k].astype(F32)).astype(BF16)
                lall[p, here_rows, at] = value
    pl.semaphore_wait(barrier, len(peers))

    def slot(p, chip, which):
        return lall.at[p, pl.ds(pl.multiple_of((2 * chip + which) * width, width), width)]

    def to_chip(src, p, chip, sgn, h):
        return remote(src, slot(p, chip, core), ss_z.at[(1 - sgn) // 2, h, p], rs_z.at[chip, p],
                      device(z + sgn, core, q))

    def to_partner(src, p, chip):
        return remote(src, slot(p, chip, core), ss_p.at[chip, p], rs_p.at[chip, p], partner)

    def inside(chip):
        return jnp.logical_and(chip >= 0, chip < CHIPS)

    for p in range(local):
        for sgn in (1, -1):
            @pl.when(inside(z + sgn))
            def _():
                to_chip(slot(p, z, core), p, z, sgn, 0).start()
    for p in range(local):
        to_partner(slot(p, z, core), p, z).start()
    inv_copy.wait()

    def far_copy(p, chip):
        to, rows = (1, half * 2 * width) if chip == 0 else (CHIPS - 2, 0)
        return remote(inv_ref.at[p, pl.ds(rows, half * 2 * width)], far.at[p], ss_far.at[p], rs_far.at[p],
                      device(to, core, q))

    if lean:
        for chip in (0, CHIPS - 1):
            @pl.when(z == chip)
            def _():
                for p in range(local):
                    far_copy(p, chip).start()

    poles = [order_ref[q * local + p] for p in range(local)]
    w_re = [weight_ref[0, poles[p]] for p in range(local)]
    w_im = [weight_ref[1, poles[p]] for p in range(local)]

    def column(p, a):
        return slot(p, z, core) if lean else col_ref.at[p, a]

    def part_copy(t):
        return remote(wfull.at[t, :, other], wrecv.at[t], ss_wp.at[t], rs_wp.at[t], partner)

    def pole_copy(o):
        to = lax.rem(q + o, n)
        return remote(wacc.at[to], wpole.at[o - 1], ss_wq.at[o - 1], rs_wq.at[o - 1], device(z, core, to))

    def join_cores(o):
        t = lax.rem(q + o, n)
        part_copy(t).wait_recv()
        wacc[t] = wfull[t, :, core] + wrecv[t]
        if o:
            pole_copy(o).start()

    shifts = list(range(1, n)) + [0]
    for place, o in enumerate(shifts):
        t = lax.rem(q + o, n)
        total = None
        for p in range(local):
            product = None
            for a in range(rg):
                block = column(p, a)
                re = block[:, pl.ds(pl.multiple_of(t * cw, 128), cw)]
                im = block[:, pl.ds(pl.multiple_of(span + t * cw, 128), cw)]
                real_form = jnp.concatenate(
                    [jnp.concatenate([re, im], axis=1), jnp.concatenate([-im, re], axis=1)], axis=0)
                term = jnp.dot(inv_ref[p, :, 2 * width * a:2 * width * (a + 1)], real_form,
                               preferred_element_type=F32)
                product = term if product is None else product + term
            term = w_im[p] * product[:, cw:] - w_re[p] * product[:, :cw]
            total = term if total is None else total + term
        wfull[t] = total.reshape(CHIPS, 2, width, cw)
        part_copy(t).start()
        if place:
            join_cores(shifts[place - 1])

    def middle(chip):
        return jnp.logical_and(chip >= 1, chip < CHIPS - 1)

    def takes(chip, h):
        if lean and h > 1:
            return jnp.logical_and(inside(chip), middle(z)) if h == 2 else False
        return inside(chip)

    def passes_on(sgn, h):
        if lean:
            return middle(z + sgn) if h == 1 else False
        return inside(z + sgn) if h < CHIPS - 1 else False

    every = range(local)

    def hop(h, ps=every):
        for p in ps:
            for sgn in (1, -1):
                chip = z - sgn * h

                @pl.when(takes(chip, h))
                def _():
                    here = slot(p, chip, core)
                    remote(here, here, ss_p.at[chip, p], rs_z.at[chip, p], partner).wait_recv()
                    if passes_on(sgn, h) is not False:
                        @pl.when(passes_on(sgn, h))
                        def _():
                            to_chip(here, p, chip, sgn, h).start()
                    to_partner(here, p, chip).start()

    def accumulate(chip, fresh, ps=every):
        rows = pl.ds(pl.multiple_of(chip * 2 * width, 2 * width), 2 * width)
        for p in ps:
            theirs = slot(p, chip, other)
            remote(theirs, theirs, ss_p.at[chip, p], rs_p.at[chip, p], partner).wait_recv()
            for a in range(rg):
                at = slice(2 * width * a, 2 * width * (a + 1))
                term = dot00(inv_ref[p, rows, at], lall[p, rows, :])
                gram[p, at, :] = term if fresh else gram[p, at, :] + term

    def gather(h, ps=every):
        for sgn in (1, -1):
            chip = z - sgn * h

            @pl.when(takes(chip, h))
            def _():
                accumulate(chip, False, ps)

    def line_copy(src, dst, send, recv, o):
        to = lax.rem(z + o, CHIPS)
        return remote(src.at[to], dst.at[o - 1], send.at[o - 1], recv.at[o - 1], device(to, core, q))

    hop(1)
    join_cores(0)
    accumulate(z, True)
    gather(1)

    per_width = width // piece

    def add_traces(fresh, p, upper, lower, block):
        m_re = upper[:, :span] - lower[:, span:]
        m_im = lower[:, :span] + upper[:, span:]
        n_re = w_re[p] * m_re - w_im[p] * m_im
        n_im = w_re[p] * m_im + w_im[p] * m_re
        both = jnp.concatenate([n_re, -n_im], axis=0)
        high = both.astype(BF16)
        low = (both - high.astype(F32)).astype(BF16)
        for k in range(sn):
            at = slice(k * width, (k + 1) * width)
            left = jnp.concatenate([block[:, at], block[:, span + k * width:span + (k + 1) * width]], axis=0)
            term = dot00(left, jnp.concatenate([high[:, at], low[:, at]], axis=1))
            term = term[:, :width] + term[:, width:]
            tt[k] = term if fresh else tt[k] + term

    def own_traces(p):
        for a in range(rg):
            base = 2 * width * a
            add_traces(p == 0 and a == 0, p, gram[p, base:base + width, :],
                       gram[p, base + width:base + 2 * width, :], column(p, a))

    def reduce_density():
        for o in range(1, n):
            pole_copy(o).wait_recv()
        wsum[...] = wacc[q] + functools.reduce(lambda x, y: x + y, [wpole[o] for o in range(n - 1)])
        for o in range(1, CHIPS):
            line_copy(wsum, wz, ss_wz, rs_wz, o).start()

    if lean:
        for p in range(local):
            hop(2, [p])
            gather(2, [p])
            own_traces(p)
            for near in (1, CHIPS - 2):
                @pl.when(z == near)
                def _():
                    end, base = (0, half) if near == 1 else (CHIPS - 1, 0)
                    rows = slice(base * 2 * width, (base + half) * 2 * width)
                    far_copy(p, end).wait_recv()
                    far_gram[p] = dot00(far[p], lall[p, rows, :])
                    add_traces(False, p, far_gram[p, :width, :], far_gram[p, width:, :], slot(p, end, core))
            if p == 0:
                reduce_density()
    else:
        hop(2)
        reduce_density()
        gather(2)
        hop(3)
        gather(3)
        for p in range(local):
            own_traces(p)
    for k in range(sn):
        trace = tt[k].T
        for g in range(k * per_width, (k + 1) * per_width):
            off = g % per_width * piece
            tbuf[g % PC // 2, g % 2, g // PC] = trace[off:off + piece]
    trace_copy = remote(tbuf.at[:, other], trecv, ss_tp.at[0], rs_tp.at[0], partner)
    trace_copy.start()

    for o in range(1, CHIPS):
        line_copy(wsum, wz, ss_wz, rs_wz, o).wait_recv()
    rows = wsum[z] + functools.reduce(lambda x, y: x + y, [wz[o] for o in range(CHIPS - 1)])
    for j in range(cw // width):
        at = slice(j * width, (j + 1) * width)
        dens_ref[:, at] = rows[:, at] * mask_ref[0, q * (cw // width) + j].astype(F32)

    trace_copy.wait_recv()
    tacc[...] = tbuf[:, core] + trecv[...]
    for o in range(1, CHIPS):
        line_copy(tacc, tz, ss_tz, rs_tz, o).start()
    for o in range(1, CHIPS):
        line_copy(tacc, tz, ss_tz, rs_tz, o).wait_recv()
    summed = tacc[z] + functools.reduce(lambda x, y: x + y, [tz[o] for o in range(CHIPS - 1)])
    if rg > 1:
        dout_ref[...] = summed.reshape(rg * piece, width)
    else:
        summed = summed.reshape(piece, width)
        for p in range(local):
            summed = summed + w_re[p] * diag_ref[p, :, :width] - w_im[p] * diag_ref[p, :, width:]
        narrow = width // n
        summed = summed.T
        for t in range(n):
            tsum[t] = summed[t * narrow:(t + 1) * narrow]

        def last_copy(o):
            to = lax.rem(q + o, n)
            return remote(tsum.at[to], tpole.at[o - 1], ss_tq.at[o - 1], rs_tq.at[o - 1], device(z, core, to))

        for o in range(1, n):
            last_copy(o).start()
        for o in range(1, n):
            last_copy(o).wait_recv()
        dout_ref[...] = tsum[q] + functools.reduce(lambda x, y: x + y, [tpole[o] for o in range(n - 1)])
        for o in range(1, n):
            last_copy(o).wait_send()

    for p in range(local):
        to_partner(slot(p, z, core), p, z).wait_send()
        for sgn in (1, -1):
            @pl.when(inside(z + sgn))
            def _():
                to_chip(slot(p, z, core), p, z, sgn, 0).wait_send()
            for h in range(1, half + 1 if lean else CHIPS):
                chip = z - sgn * h

                @pl.when(takes(chip, h))
                def _():
                    here = slot(p, chip, core)
                    if passes_on(sgn, h) is not False:
                        @pl.when(passes_on(sgn, h))
                        def _():
                            to_chip(here, p, chip, sgn, h).wait_send()
                    to_partner(here, p, chip).wait_send()
    if lean:
        for chip in (0, CHIPS - 1):
            @pl.when(z == chip)
            def _():
                for p in range(local):
                    far_copy(p, chip).wait_send()
    for t in range(n):
        part_copy(t).wait_send()
    for o in range(1, n):
        pole_copy(o).wait_send()
    trace_copy.wait_send()
    for o in range(1, CHIPS):
        line_copy(wsum, wz, ss_wz, rs_wz, o).wait_send()
        line_copy(tacc, tz, ss_tz, rs_tz, o).wait_send()


def land(*arrays):
    def move(*refs):
        for source, target in zip(refs[:len(arrays)], refs[len(arrays):]):
            target[...] = source[...]

    return pl.pallas_call(move, out_shape=[jax.ShapeDtypeStruct(x.shape, x.dtype) for x in arrays])(*arrays)


def per_device(inverse_blocks, panel_blocks, ancestor_mask, diag_inverse, pole_weights, pole_order):
    local, width = panel_blocks.shape[:2]
    sn = ancestor_mask.shape[1]
    span = sn * width
    n = lax.axis_size("pole")
    rg = lax.axis_size("blk") // PC
    cw = span // n
    piece = span // (PC * rg)
    me = lax.axis_index("blk")
    mask_row = jnp.broadcast_to(ancestor_mask[0].astype(BF16)[None, :, None], (2, sn, width)).reshape(2 * span)
    own_panel = panel_blocks * mask_row[None, None, :] if rg > 1 else panel_blocks
    arrays = [pole_weights.T, pole_order, ancestor_mask, inverse_blocks, own_panel]
    if rg > 1:
        pieces = [own_panel] + [from_behind(own_panel, "blk", o * PC) for o in range(1, rg)]
        arrays.append(jnp.roll(jnp.stack(pieces[::-1], axis=1), me // PC + 1, axis=1))
    arrays.append(diag_inverse)
    smem = pl.BlockSpec(memory_space=pltpu.SMEM)
    vmem = pl.BlockSpec(memory_space=pltpu.VMEM)
    diag_shape = (width // n, piece) if rg == 1 else (rg * piece, width)
    dma = pltpu.SemaphoreType.DMA
    density, diag = pl.pallas_call(
        functools.partial(kernel, (n, rg, local, width, sn)),
        out_shape=(jax.ShapeDtypeStruct((width, cw), F32), jax.ShapeDtypeStruct(diag_shape, F32)),
        in_specs=[smem] * 3 + [pl.BlockSpec(memory_space=pl.ANY)] + [vmem] * (len(arrays) - 4),
        out_specs=(vmem, vmem),
        scratch_shapes=[
            pltpu.VMEM(inverse_blocks.shape, BF16), dma((1,)),
            pltpu.VMEM((local, CHIPS // 2 * 2 * width, 2 * width) if rg == 1 else (8, 128), BF16),
            pltpu.VMEM((local, 2 * width, 2 * span) if rg == 1 else (8, 128), F32),
            pltpu.VMEM((sn, width, width), F32),
            dma((local,)), dma((local,)),
            pltpu.VMEM((local, PC * width, 2 * span), BF16),
            pltpu.VMEM((local, rg * 2 * width, 2 * span), F32),
            pltpu.VMEM((n, CHIPS, 2, width, cw), F32),
            pltpu.VMEM((n, CHIPS, width, cw), F32),
            pltpu.VMEM((n, CHIPS, width, cw), F32),
            pltpu.VMEM((n - 1, CHIPS, width, cw), F32),
            pltpu.VMEM((CHIPS, width, cw), F32),
            pltpu.VMEM((CHIPS - 1, width, cw), F32),
            pltpu.VMEM((CHIPS, 2, rg, piece, width), F32),
            pltpu.VMEM((CHIPS, rg, piece, width), F32),
            pltpu.VMEM((CHIPS, rg, piece, width), F32),
            pltpu.VMEM((CHIPS - 1, rg, piece, width), F32),
            pltpu.VMEM((n, width // n, piece), F32),
            pltpu.VMEM((n - 1, width // n, piece), F32),
            dma((2, CHIPS - 1, local)), dma((CHIPS, local)), dma((CHIPS, local)), dma((CHIPS, local)),
            dma((n,)), dma((n,)), dma((n - 1,)), dma((n - 1,)), dma((CHIPS - 1,)), dma((CHIPS - 1,)),
            dma((1,)), dma((1,)), dma((CHIPS - 1,)), dma((CHIPS - 1,)), dma((n - 1,)), dma((n - 1,)),
        ],
        compiler_params=pltpu.CompilerParams(collective_id=0, has_side_effects=True),
    )(*arrays)
    if rg > 1:
        groups = [[r * PC + b for r in range(rg)] for b in range(PC)]
        diag = lax.psum_scatter(diag, "blk", scatter_dimension=0, axis_index_groups=groups, tiled=True)
        chosen = lax.dynamic_slice_in_dim(pole_order, lax.axis_index("pole") * local, local, 0)
        pairs = pole_weights[chosen]
        diag = diag + jnp.sum(
            pairs[:, 0, None, None] * diag_inverse[..., :width] - pairs[:, 1, None, None] * diag_inverse[..., width:],
            axis=0)
        diag = lax.psum_scatter(diag, "pole", scatter_dimension=1, tiled=True)
    else:
        density, diag = land(density, diag)
        diag = diag.T
    return density, diag


def solution(mesh):
    placed = (
        P("pole", "blk", None),
        P("pole", "blk", None),
        P("blk", None),
        P("pole", "blk", None),
        P(),
        P(),
    )
    return jax.shard_map(
        per_device,
        mesh=mesh,
        in_specs=placed,
        out_specs=(P("blk", "pole"), P("blk", "pole")),
        check_vma=False,
    )
```
